256 devices in a mesh: expert: 128 (over z, y, x), dp: 2 (over core).
Axes of the slice: x: 4, y: 4, z: 8, core: 2. Of those that a mesh axis runs over, the one named last changes fastest.
Arguments:
- hidden_in: float32 [12288, 2048], P(('expert', 'dp')), may hold values from -6 to 6
- out_grad: float32 [12288, 2048], P(('expert', 'dp')), may hold values from -6 to 6
- route_prob: float32 [12288, 8], P(('expert', 'dp')), may hold values from 0.03 to 0.6
- route_ids: int32 [12288, 8], P(('expert', 'dp')), may hold values from 0 to 127, all different within a row; in each aligned block of 48 rows (0 to 47, 48 to 95, ...) at most 4 rows name the same one
- w_gate: bfloat16 [128, 2048, 768], P('expert', None, 'dp'), may hold values from -0.125 to 0.125
- w_up: bfloat16 [128, 2048, 768], P('expert', None, 'dp'), may hold values from -0.125 to 0.125
- w_down: bfloat16 [128, 2048, 768], P('expert', None, 'dp'), may hold values from -0.21875 to 0.21875
Outputs:
- input_grad: float32 [12288, 2048], P(('expert', 'dp'))
- grad_gate: bfloat16 [128, 2048, 768], P('expert', None, 'dp')
- grad_up: bfloat16 [128, 2048, 768], P('expert', None, 'dp')
- grad_down: bfloat16 [128, 2048, 768], P('expert', None, 'dp')
The draws below stay inside these ranges and needn't reach their ends.
Inputs may be any that keep to these rules, and one draw needn't show every extreme that they name: `route_ids`: each row names 8 different experts. Among the 48 tokens of one device no expert is named more than 4 times; in every draw some expert is named exactly 4 times by the tokens of some device.
All inputs are finite; a program needn't handle non-finite values.
Results may differ from the reference program's by a relative error of at most 0.0089.
Values may be sent and summed in bfloat16 or wider, within the bound.
No kernel may reach another device: no remote copies, remote signals or barrier semaphores. Data moves between devices by JAX's collectives and lax.ppermute only.
A program may use at most 128 MiB of HBM per device.

```python
import math
import jax
import jax.numpy as jnp
import numpy as np
from jax import lax

D = 2048
FF = 768
TOP = 8
TOK_DEV = 48
EXPERTS = 128
CAP = 4
TOKENS = 12288
N_EXPERT = 128
N_DP = 2


def block_scale(rng, extent, pieces, least, largest):
    factor_of, own = 1.0, jax.random.fold_in(rng, 6)
    for position, blocks in pieces:
        steps = jnp.exp(jax.random.uniform(jax.random.fold_in(own, position), (blocks,), jnp.float32, least / len(pieces), largest / len(pieces)))
        factor_of = factor_of * jnp.repeat(steps, extent[position] // blocks).reshape([-1 if axis == position else 1 for axis in range(len(extent))])
    return factor_of


def routed_block(stream_key, own, number, rows, count, top, reach, slope):
    sequence = jax.random.permutation(stream_key, count)
    crowded, ordinary = shares(count, rows * top, reach, slope, True), shares(count, rows * top, reach, slope, False)
    places = jnp.arange(count)

    def named(tallies, turn):
        used = int((tallies > 0).sum())
        fixed = max(1, used // 4)
        shifted = fixed + (places - fixed + turn * (used - fixed)) % max(1, count - fixed)
        return jnp.zeros((count,), jnp.int32).at[sequence[jnp.where(places < fixed, places, shifted)]].set(jnp.asarray(tallies, jnp.int32))

    tallies = jnp.where(number % 4 == 0, named(crowded, number // 4), named(ordinary, number - number // 4 - 1))
    mixed = jax.random.permutation(jax.random.fold_in(own, 3), count)
    donor, receiver = mixed[0:count // 2 * 2:2], mixed[1:count // 2 * 2:2]
    room = jnp.minimum(tallies[donor] - 1, reach - tallies[receiver]) // 2
    room = jnp.where((donor == sequence[0]) | (receiver == sequence[0]) | (tallies[receiver] == 0), 0, jnp.maximum(room, 0))
    shifted = jax.random.randint(jax.random.fold_in(own, 4), (count // 2,), 0, 1 << 20) % (room + 1)
    tallies = tallies.at[donor].add(-shifted).at[receiver].add(shifted)
    members = jnp.searchsorted(jnp.cumsum(tallies), jnp.arange(rows * top), side="right").astype(jnp.int32)
    table = members.reshape(top, rows).T
    table = table[jax.random.permutation(jax.random.fold_in(own, 1), rows)]
    turn = jax.random.randint(jax.random.fold_in(own, 2), (rows, 1), 0, top)
    return jnp.take_along_axis(table, (jnp.arange(top)[None, :] + turn) % top, axis=1)


def shares(count, total, most, slope, full):
    portions = [(1 << 20) // math.isqrt(grade ** slope) + 1 for grade in range(1, count + 1)]
    largest = most if full else min(most, max(-(-total // count), total * portions[0] // sum(portions)))
    least = 1 if total - largest >= count - 1 else 0
    counts, rest = [largest] + [least] * (count - 1), total - largest - least * (count - 1)
    while rest > 0:
        free = [i for i in range(1, count) if counts[i] < largest] or [i for i in range(1, count) if counts[i] < most]
        mass, budget = sum([portions[i] for i in free]), rest
        for i in free:
            extra = min(most - counts[i], max(1, budget * portions[i] // mass), rest)
            counts[i] = counts[i] + extra
            rest = rest - extra
    return np.array(counts)


def centred(rng, dims, spread, bound, split=(), held_as=jnp.bfloat16):
    array = jax.random.normal(rng, dims, jnp.float32) * spread
    if len(split) > 0:
        array = block_scale(rng, dims, split, -0.22, 0.18) * array
    return jnp.clip(array, min=-bound, max=bound).astype(held_as)


def setup_inputs(seed: int = 0) -> dict:
    splits = jax.random.split(jax.random.key(seed), 8)
    hidden_in = centred(splits[0], (TOKENS, D), 1.0, 6.0, ((0, 256),), jnp.float32)
    out_grad = centred(splits[1], (TOKENS, D), 1.0, 6.0, ((0, 256),), jnp.float32)
    route_prob = jnp.clip(jnp.exp(math.log(0.6) - 2.9957323 * jax.random.uniform(splits[2], (TOKENS, TOP), jnp.float32) ** block_scale(splits[2], (TOKENS, TOP), ((0, 256),), -0.2, 0.2)), 0.03, 0.6)
    route_ids_keys = jax.random.split(jax.random.fold_in(splits[3], 1), TOKENS // TOK_DEV)
    route_ids_turns = jax.random.permutation(jax.random.fold_in(splits[3], 3), TOKENS // TOK_DEV)
    route_ids = jax.vmap(lambda own, number: routed_block(jax.random.fold_in(splits[3], 2), own, number, TOK_DEV, EXPERTS, TOP, CAP, 2))(route_ids_keys, route_ids_turns).reshape((TOKENS, TOP))
    w_gate = centred(splits[4], (EXPERTS, D, FF), D ** -0.5, 0.125, ((0, 128), (2, 2)))
    w_up = centred(splits[5], (EXPERTS, D, FF), D ** -0.5, 0.125, ((0, 128), (2, 2)))
    w_down = centred(splits[6], (EXPERTS, D, FF), FF ** -0.5, 0.21875, ((0, 128), (2, 2)))
    return {"hidden_in": hidden_in, "out_grad": out_grad, "route_prob": route_prob, "route_ids": route_ids, "w_gate": w_gate, "w_up": w_up, "w_down": w_down}


def expert_grads(xs, gs, ps, wg, wu, wd):
    gate = jnp.dot(xs, wg, preferred_element_type=jnp.float32)
    upper = jnp.dot(xs, wu, preferred_element_type=jnp.float32)
    sig = jax.nn.sigmoid(gate)
    act = gate * sig
    hidden = (act * upper).astype(jnp.bfloat16)
    grad_out = (ps.astype(jnp.float32)[:, None] * gs.astype(jnp.float32)).astype(jnp.bfloat16)
    grad_hid = jnp.dot(grad_out, wd, preferred_element_type=jnp.float32)
    grad_gate = (grad_hid * upper * sig * (1.0 + gate * (1.0 - sig))).astype(jnp.bfloat16)
    grad_upper = (grad_hid * act).astype(jnp.bfloat16)
    back = lax.dot_general(grad_gate, wg, (((1,), (1,)), ((), ())), preferred_element_type=jnp.float32)
    back = back + lax.dot_general(grad_upper, wu, (((1,), (1,)), ((), ())), preferred_element_type=jnp.float32)
    part_gate = lax.dot_general(xs, grad_gate, (((0,), (0,)), ((), ())), preferred_element_type=jnp.float32)
    part_upper = lax.dot_general(xs, grad_upper, (((0,), (0,)), ((), ())), preferred_element_type=jnp.float32)
    part_down = lax.dot_general(grad_out, hidden, (((0,), (0,)), ((), ())), preferred_element_type=jnp.float32)
    return back, (part_gate, part_upper, part_down)


def reference(hidden_in, out_grad, route_prob, route_ids, w_gate, w_up, w_down):
    pairs_all = TOKENS * TOP
    devices = N_EXPERT * N_DP
    per_dev = TOK_DEV * TOP
    ids_dev = route_ids.reshape(devices, per_dev)
    onehot = (ids_dev[:, :, None] == jnp.arange(EXPERTS, dtype=jnp.int32)[None, None, :]).astype(jnp.int32)
    before = jnp.cumsum(onehot, axis=1) - onehot
    rank = jnp.sum(before * onehot, axis=2).reshape(-1)
    flat_ids = route_ids.reshape(-1)
    pair_idx = jnp.arange(pairs_all, dtype=jnp.int32)
    device = pair_idx // per_dev
    source = device // N_DP
    group = device % N_DP
    slot = ((flat_ids * N_DP + group) * N_EXPERT + source) * CAP + rank
    table = jnp.full((EXPERTS * N_DP * N_EXPERT * CAP,), pairs_all, jnp.int32).at[slot].set(pair_idx)
    table = table.reshape(EXPERTS, N_DP, N_EXPERT * CAP)
    token_of = jnp.where(table < pairs_all, table // TOP, TOKENS).astype(jnp.int32)
    x_pad = jnp.concatenate([hidden_in.astype(jnp.bfloat16), jnp.zeros((1, D), jnp.bfloat16)], axis=0)
    g_pad = jnp.concatenate([out_grad.astype(jnp.bfloat16), jnp.zeros((1, D), jnp.bfloat16)], axis=0)
    p_pad = jnp.concatenate([route_prob.astype(jnp.bfloat16).reshape(-1), jnp.zeros((1,), jnp.bfloat16)], axis=0)

    def per_expert(carry, expert):
        totals = [jnp.zeros((D, FF), jnp.float32) for _ in range(3)]
        for group_idx in range(N_DP):
            tok = token_of[expert, group_idx]
            xs = x_pad[tok]
            gs = g_pad[tok]
            ps = p_pad[table[expert, group_idx]]
            back, parts = expert_grads(xs, gs, ps, w_gate[expert], w_up[expert], w_down[expert])
            carry = carry.at[tok].add(back.astype(jnp.bfloat16).astype(jnp.float32))
            totals = [tot + part.astype(jnp.bfloat16).astype(jnp.float32) for tot, part in zip(totals, parts)]
        return carry, tuple(tot.astype(jnp.bfloat16) for tot in totals)

    start = jnp.zeros((TOKENS + 1, D), jnp.float32)
    final, grads = lax.scan(per_expert, start, jnp.arange(EXPERTS, dtype=jnp.int32))
    return (final[:TOKENS], grads[0], grads[1], grads[2])
```

```python
import jax
import jax.numpy as jnp
from jax import lax
from jax.sharding import PartitionSpec as P

F32 = jnp.float32
BF16 = jnp.bfloat16


def mm(a, b, dims):
    return lax.dot_general(a, b, ((dims[0], dims[1]), ((), ())), preferred_element_type=F32)


def per_device(hidden_in, out_grad, route_prob, route_ids, w_gate, w_up, w_down):
    tok_count, top_count = route_ids.shape
    width = hidden_in.shape[1]
    peers = lax.axis_size("expert")
    half = w_gate.shape[2]
    slot_cap = max(2, 12 * tok_count // peers)
    total_slots = peers * slot_cap
    swap = [(0, 1), (1, 0)]

    ids_t = route_ids.T
    prob_t = route_prob.T.astype(BF16).astype(F32)
    slot = lax.broadcasted_iota(jnp.int32, (total_slots, tok_count), 0)
    slot_expert = slot // slot_cap
    named = jnp.zeros((total_slots, tok_count), F32)
    prob = jnp.zeros((total_slots, tok_count), F32)
    for k in range(top_count):
        hit = slot_expert == ids_t[k][None, :]
        named = jnp.where(hit, 1.0, named)
        prob = jnp.where(hit, prob_t[k][None, :], prob)
    earlier = (
        lax.broadcasted_iota(jnp.int32, (tok_count, tok_count), 0)
        < lax.broadcasted_iota(jnp.int32, (tok_count, tok_count), 1)
    ).astype(BF16)
    rank = mm(named.astype(BF16), earlier, ((1,), (0,)))
    chosen = (named > 0.0) & (rank == (slot % slot_cap).astype(F32))
    pick = chosen.astype(BF16)
    pick_prob = jnp.where(chosen, prob, 0.0).astype(BF16)

    def exchange(rows):
        out = lax.all_to_all(
            rows.reshape(peers, slot_cap, width), "expert", split_axis=0, concat_axis=0, tiled=True
        )
        return out.reshape(total_slots, width)

    send_x = mm(pick, hidden_in.astype(BF16), ((1,), (0,))).astype(BF16)
    xs = exchange(send_x)
    send_g = mm(pick_prob, out_grad.astype(BF16), ((1,), (0,))).astype(BF16)
    go = exchange(send_g)

    def both(w):
        return jnp.concatenate([w[0], lax.ppermute(w[0], "dp", swap)], axis=1)

    wg, wu, wd = both(w_gate), both(w_up), both(w_down)

    gate = mm(xs, wg, ((1,), (0,)))
    upper = mm(xs, wu, ((1,), (0,)))
    grad_hid = mm(go, wd, ((1,), (0,)))
    sig = jax.nn.sigmoid(gate)
    act = gate * sig
    hid = (act * upper).astype(BF16)
    da = (grad_hid * upper * sig * (1.0 + gate * (1.0 - sig))).astype(BF16)
    db = (grad_hid * act).astype(BF16)
    back = mm(da, wg, ((1,), (1,))) + mm(db, wu, ((1,), (1,)))
    back_b, da, db, hid, xs, go = lax.optimization_barrier((back.astype(BF16), da, db, hid, xs, go))
    returned = exchange(back_b)

    def grad(rows, hidden):
        mine = mm(rows, hidden[:, :half], ((0,), (0,))).astype(BF16)
        other = mm(rows, hidden[:, half:], ((0,), (0,))).astype(BF16)
        got = lax.ppermute(other, "dp", swap)
        return (mine.astype(F32) + got.astype(F32)).astype(BF16)[None]

    grads = (grad(xs, da), grad(xs, db), grad(go, hid))
    input_grad = mm(pick, returned, ((0,), (0,)))
    return (input_grad, grads[0], grads[1], grads[2])


def solution(mesh):
    tok = P(("expert", "dp"), None)
    wts = P("expert", None, "dp")
    return jax.shard_map(
        per_device,
        mesh=mesh,
        in_specs=(tok, tok, tok, tok, wts, wts, wts),
        out_specs=(tok, wts, wts, wts),
        check_vma=False,
    )
```

```python
import jax
import jax.numpy as jnp
from jax import lax
from jax.sharding import Mesh, PartitionSpec as P

F32 = jnp.float32
BF16 = jnp.bfloat16
PLANE = 16
LANES = 128


def mm(a, b, dims):
    return lax.dot_general(a, b, ((dims[0], dims[1]), ((), ())), preferred_element_type=F32)


def before(count, block):
    i = lax.broadcasted_iota(jnp.int32, (count, count), 0)
    j = lax.broadcasted_iota(jnp.int32, (count, count), 1)
    return ((i < j) & (i // block == j // block)).astype(BF16)


def named_by(expert, ids_t, prob_t):
    named = jnp.zeros(jnp.broadcast_shapes(expert.shape, (1, ids_t.shape[1])), F32)
    prob = named
    for k in range(ids_t.shape[0]):
        hit = expert == ids_t[k][None, :]
        named = jnp.where(hit, 1.0, named)
        if prob_t is not None:
            prob = jnp.where(hit, prob_t[k][None, :], prob)
    return named, prob


def along_z(rows, depth):
    up = [(i, (i + 1) % depth) for i in range(depth)]
    down = [(i, (i - 1) % depth) for i in range(depth)]
    below = above = rows
    blocks, offsets = [rows], [0]
    for step in range(1, depth // 2 + 1):
        below = lax.ppermute(below, "z", up)
        blocks.append(below)
        offsets.append(depth - step)
        if step < depth - step:
            above = lax.ppermute(above, "z", down)
            blocks.append(above)
            offsets.append(step)
    return jnp.concatenate(blocks, axis=0), offsets


def per_device(hidden_in, out_grad, route_prob, route_ids, w_gate, w_up, w_down):
    tok_count, top_count = route_ids.shape
    width = hidden_in.shape[1]
    depth = lax.axis_size("z")
    peers = depth * PLANE
    half = w_gate.shape[2]
    slot_cap = max(2, 12 * tok_count // peers)
    total_slots = peers * slot_cap
    swap = [(0, 1), (1, 0)]

    meta = jnp.concatenate(
        [
            hidden_in.astype(BF16),
            route_ids.astype(BF16),
            route_prob.astype(BF16),
            jnp.zeros((tok_count, LANES - 2 * top_count), BF16),
        ],
        axis=1,
    )
    column, came_from = along_z(meta, depth)
    small = column[:, width:].T.astype(F32)
    g_rows, _ = lax.optimization_barrier((out_grad.astype(BF16), small))
    g_column, _ = along_z(g_rows, depth)

    col_toks = depth * tok_count
    col_ids = small[:top_count].astype(jnp.int32)
    col_prob = small[top_count : 2 * top_count]
    plane_expert = lax.axis_index("z") * PLANE + lax.broadcasted_iota(jnp.int32, (PLANE, 1), 0)
    named, prob = named_by(plane_expert, col_ids, col_prob)
    rank = mm(named.astype(BF16), before(col_toks, tok_count), ((1,), (0,)))
    rank = jnp.where(named > 0.0, rank, -1.0)
    block = depth * slot_cap
    row = lax.broadcasted_iota(jnp.int32, (1, block, col_toks), 1)
    col = lax.broadcasted_iota(jnp.int32, (1, block, col_toks), 2)
    source = jnp.zeros_like(col)
    for place, offset in enumerate(came_from):
        source = jnp.where(col // tok_count == place, (lax.axis_index("z") + offset) % depth, source)
    chosen = (rank[:, None, :] == (row % slot_cap).astype(F32)) & (row // slot_cap == source)
    pick_x = chosen.astype(BF16).reshape(total_slots, col_toks)
    pick_g = jnp.where(chosen, prob[:, None, :], 0.0).astype(BF16).reshape(total_slots, col_toks)

    def in_plane(rows):
        return lax.all_to_all(
            rows.reshape(PLANE, block, width), ("y", "x"), split_axis=0, concat_axis=0, tiled=True
        ).reshape(total_slots, width)

    xs = in_plane(mm(pick_x, column[:, :width], ((1,), (0,))).astype(BF16))
    send_g = mm(pick_g, g_column, ((1,), (0,))).astype(BF16)
    send_g, xs = lax.optimization_barrier((send_g, xs))
    go = in_plane(send_g)

    slot = lax.broadcasted_iota(jnp.int32, (total_slots, 1), 0)
    peer = slot // slot_cap
    slot_expert = (peer % depth) * PLANE + peer // depth
    named, _ = named_by(slot_expert, route_ids.T, None)
    rank = mm(named.astype(BF16), before(tok_count, tok_count), ((1,), (0,)))
    pick = ((named > 0.0) & (rank == (slot % slot_cap).astype(F32))).astype(BF16)

    def exchange(rows):
        out = lax.all_to_all(
            rows.reshape(peers, slot_cap, width), ("y", "x", "z"), split_axis=0, concat_axis=0, tiled=True
        )
        return out.reshape(total_slots, width)

    def both(w):
        return jnp.concatenate([w[0], lax.ppermute(w[0], "dp", swap)], axis=1)

    wg, wu, wd = both(w_gate), both(w_up), both(w_down)

    gate = mm(xs, wg, ((1,), (0,)))
    upper = mm(xs, wu, ((1,), (0,)))
    grad_hid = mm(go, wd, ((1,), (0,)))
    sig = jax.nn.sigmoid(gate)
    act = gate * sig
    hid = (act * upper).astype(BF16)
    da = (grad_hid * upper * sig * (1.0 + gate * (1.0 - sig))).astype(BF16)
    db = (grad_hid * act).astype(BF16)
    back = mm(da, wg, ((1,), (1,))) + mm(db, wu, ((1,), (1,)))
    back_b, da, db, hid, xs, go = lax.optimization_barrier((back.astype(BF16), da, db, hid, xs, go))
    returned = exchange(back_b)

    def grad(rows, hidden):
        mine = mm(rows, hidden[:, :half], ((0,), (0,))).astype(BF16)
        other = mm(rows, hidden[:, half:], ((0,), (0,))).astype(BF16)
        got = lax.ppermute(other, "dp", swap)
        return (mine.astype(F32) + got.astype(F32)).astype(BF16)[None]

    grads = (grad(xs, da), grad(xs, db), grad(go, hid))
    input_grad = mm(pick, returned, ((0,), (0,)))
    return (input_grad, grads[0], grads[1], grads[2])


def solution(mesh):
    grid = Mesh(mesh.devices.reshape(-1, 4, 4, 2), ("z", "y", "x", "dp"))
    tok = P(("z", "y", "x", "dp"), None)
    wts = P(("z", "y", "x"), None, "dp")
    return jax.shard_map(
        per_device,
        mesh=grid,
        in_specs=(tok, tok, tok, tok, wts, wts, wts),
        out_specs=(tok, wts, wts, wts),
        check_vma=False,
    )
```

```python
import jax
import jax.numpy as jnp
from jax import lax
from jax.experimental import pallas as pl
from jax.experimental.pallas import tpu as pltpu
from jax.sharding import Mesh, PartitionSpec as P

F32 = jnp.float32
BF16 = jnp.bfloat16
PLANE = 16
LANES = 128
SCOPED = 8 << 20
IN_HBM = pl.BlockSpec(memory_space=pltpu.HBM)
IN_VMEM = pl.BlockSpec(memory_space=pltpu.VMEM)


def mm(a, b, dims):
    return lax.dot_general(a, b, ((dims[0], dims[1]), ((), ())), preferred_element_type=F32)


def before(count, block):
    i = lax.broadcasted_iota(jnp.int32, (count, count), 0)
    j = lax.broadcasted_iota(jnp.int32, (count, count), 1)
    return ((i < j) & (i // block == j // block)).astype(BF16)


def named_by(expert, ids_t, prob_t):
    named = jnp.zeros(jnp.broadcast_shapes(expert.shape, (1, ids_t.shape[1])), F32)
    prob = named
    for k in range(ids_t.shape[0]):
        hit = expert == ids_t[k][None, :]
        named = jnp.where(hit, 1.0, named)
        if prob_t is not None:
            prob = jnp.where(hit, prob_t[k][None, :], prob)
    return named, prob


def along_z(rows, depth):
    up = [(i, (i + 1) % depth) for i in range(depth)]
    down = [(i, (i - 1) % depth) for i in range(depth)]
    below = above = rows
    blocks, offsets = [rows], [0]
    for step in range(1, depth // 2 + 1):
        below = lax.ppermute(below, "z", up)
        blocks.append(below)
        offsets.append(depth - step)
        if step < depth - step:
            above = lax.ppermute(above, "z", down)
            blocks.append(above)
            offsets.append(step)
    return blocks, offsets


def iota(shape, dim):
    return lax.broadcasted_iota(jnp.int32, shape, dim)


def prepare(x, ids_t, prob_t):
    toks, width = x.shape
    top = ids_t.shape[0]

    def body(x_ref, ids_ref, prob_ref, out_ref):
        out_ref[:, :width] = x_ref[...].astype(BF16)
        small = jnp.concatenate([ids_ref[...].astype(F32), prob_ref[...]], axis=0).astype(BF16)
        place = (iota((2 * top, LANES), 0) == iota((2 * top, LANES), 1)).astype(F32).astype(BF16)
        out_ref[:, width:] = mm(small, place, ((0,), (0,))).astype(BF16)

    return pl.pallas_call(
        body,
        out_specs=IN_VMEM,
        out_shape=jax.ShapeDtypeStruct((toks, width + LANES), BF16),
        name="prepare",
    )(x, ids_t, prob_t)


def narrow(x, after):
    def body(x_ref, *refs):
        refs[-1][...] = x_ref[...].astype(BF16)

    return pl.pallas_call(
        body,
        in_specs=[IN_VMEM] * (1 + len(after)),
        out_specs=IN_VMEM,
        out_shape=jax.ShapeDtypeStruct(x.shape, BF16),
        compiler_params=pltpu.CompilerParams(vmem_limit_bytes=SCOPED),
        name="narrow",
    )(x, *after)


def fill_x(blocks, offsets, z, top, cap, width, parts, after):
    toks = blocks[0].shape[0]
    depth = len(blocks)
    cols = depth * toks
    rows = depth * cap
    slots = PLANE * rows
    chunk = width // parts

    def body(z_ref, *refs):
        out_ref, weigh_ref, pick_ref, buf_ref, sems = refs[depth + len(after) :]
        refs = refs[:depth]
        if True:
            me = z_ref[0]
            meta = jnp.concatenate([ref[:, width:] for ref in refs], axis=0)
            take = (iota((2 * top, LANES), 0) == iota((2 * top, LANES), 1)).astype(F32).astype(BF16)
            small = mm(take, meta, ((1,), (1,)))
            expert = (iota((PLANE, cols), 0) + me * PLANE).astype(F32)
            named = jnp.zeros((PLANE, cols), F32)
            prob = jnp.zeros((PLANE, cols), F32)
            for k in range(top):
                hit = small[k : k + 1] == expert
                named = jnp.where(hit, 1.0, named)
                prob = jnp.where(hit, small[top + k : top + k + 1], prob)
            i, j = iota((cols, cols), 0), iota((cols, cols), 1)
            start = jnp.zeros((cols, cols), jnp.int32)
            for b in range(1, depth):
                start = jnp.where(j >= b * toks, b * toks, start)
            earlier = jnp.where((i < j) & (i >= start), 1.0, 0.0).astype(BF16)
            rank = mm(named.astype(BF16), earlier, ((1,), (0,)))
            rank = jnp.where(named > 0.0, rank, -64.0 * depth)
            row, col = iota((rows, cols), 0), iota((rows, cols), 1)
            source = jnp.zeros((rows, cols), jnp.int32)
            for b in range(depth):
                source = jnp.where(col >= b * toks, (me + offsets[b]) & (depth - 1), source)
            wanted = (row - source * cap).astype(F32)
            for e in range(PLANE):
                chosen = (rank[e : e + 1] == wanted)
                pick_ref[e * rows : (e + 1) * rows] = jnp.where(chosen, 1.0, 0.0).astype(BF16)
                weigh_ref[e * rows : (e + 1) * rows] = jnp.where(chosen, prob[e : e + 1], 0.0).astype(BF16)

        def send(i):
            here = pl.ds(i, chunk)
            return pltpu.make_async_copy(buf_ref.at[:, here], out_ref.at[:, here], sems.at[i // chunk])

        for i in range(0, width, chunk):
            x = jnp.concatenate([ref[:, i : i + chunk] for ref in refs], axis=0)
            buf_ref[:, i : i + chunk] = mm(pick_ref[...], x, ((1,), (0,))).astype(BF16)
            send(i).start()
        for i in range(0, width, chunk):
            send(i).wait()

    return pl.pallas_call(
        body,
        in_specs=[pl.BlockSpec(memory_space=pltpu.SMEM)] + [IN_VMEM] * (depth + len(after)),
        out_specs=[IN_HBM, IN_VMEM],
        scratch_shapes=[
            pltpu.VMEM((slots, cols), BF16),
            pltpu.VMEM((slots, width), BF16),
            pltpu.SemaphoreType.DMA((parts,)),
        ],
        out_shape=[pltpu.HBM((slots, width), BF16), pltpu.VMEM((slots, cols), BF16)],
        compiler_params=pltpu.CompilerParams(vmem_limit_bytes=SCOPED),
        name="fill_x",
    )(z, *blocks, *after)


def fill_g(weigh, blocks, parts):
    toks, width = blocks[0].shape
    slots, cols = weigh.shape
    chunk = width // parts

    def body(weigh_ref, *refs):
        refs, (out_ref, buf_ref, sems) = refs[:-3], refs[-3:]

        def send(i):
            here = pl.ds(i, chunk)
            return pltpu.make_async_copy(buf_ref.at[:, here], out_ref.at[:, here], sems.at[i // chunk])

        for i in range(0, width, chunk):
            g = jnp.concatenate([ref[:, i : i + chunk] for ref in refs], axis=0)
            buf_ref[:, i : i + chunk] = mm(weigh_ref[...], g, ((1,), (0,))).astype(BF16)
            send(i).start()
        for i in range(0, width, chunk):
            send(i).wait()

    return pl.pallas_call(
        body,
        in_specs=[IN_VMEM] * (1 + len(blocks)),
        out_specs=IN_HBM,
        scratch_shapes=[pltpu.VMEM((slots, width), BF16), pltpu.SemaphoreType.DMA((parts,))],
        out_shape=pltpu.HBM((slots, width), BF16),
        compiler_params=pltpu.CompilerParams(vmem_limit_bytes=SCOPED),
        name="fill_g",
    )(weigh, *blocks)


def activations(xs, wg, wu, part):
    rows, width = xs.shape
    hidden = wg.shape[1]

    def body(x_h, wg_ref, wu_ref, act_h, slope_h, hid_h, act_ref, slope_ref, hid_ref, x_ref, sems):
        arrive = pltpu.make_async_copy(x_h, x_ref, sems.at[3])
        arrive.start()
        arrive.wait()
        for i in range(0, hidden, part):
            a = mm(x_ref[...], wg_ref[:, i : i + part], ((1,), (0,)))
            b = mm(x_ref[...], wu_ref[:, i : i + part], ((1,), (0,)))
            sig = 1.0 / (1.0 + jnp.exp(-a))
            act = a * sig
            act_ref[:, i : i + part] = act
            slope_ref[:, i : i + part] = b * sig * (1.0 + a * (1.0 - sig))
            hid_ref[:, i : i + part] = (act * b).astype(BF16)
        copies = [
            pltpu.make_async_copy(src, dst, sems.at[i])
            for i, (src, dst) in enumerate([(act_ref, act_h), (slope_ref, slope_h), (hid_ref, hid_h)])
        ]
        for copy in copies:
            copy.start()
        for copy in copies:
            copy.wait()

    return pl.pallas_call(
        body,
        in_specs=[IN_HBM, IN_VMEM, IN_VMEM],
        out_specs=[IN_HBM] * 3,
        out_shape=[
            pltpu.HBM((rows, hidden), F32),
            pltpu.HBM((rows, hidden), F32),
            pltpu.HBM((rows, hidden), BF16),
        ],
        scratch_shapes=[
            pltpu.VMEM((rows, hidden), F32),
            pltpu.VMEM((rows, hidden), F32),
            pltpu.VMEM((rows, hidden), BF16),
            pltpu.VMEM((rows, width), BF16),
            pltpu.SemaphoreType.DMA((4,)),
        ],
        compiler_params=pltpu.CompilerParams(vmem_limit_bytes=2 * SCOPED),
        name="activations",
    )(pltpu.with_memory_space_constraint(xs, pltpu.HBM), wg, wu)


def combine(pick, rows, parts):
    slots, toks = pick.shape
    peers, cap, width = rows.shape
    chunk = width // parts

    def body(pick_ref, rows_ref, out_ref):
        for i in range(0, width, chunk):
            part = rows_ref[:, :, i : i + chunk].astype(F32).reshape(slots, chunk).astype(BF16)
            out_ref[:, i : i + chunk] = mm(pick_ref[...], part, ((0,), (0,)))

    return pl.pallas_call(
        body,
        in_specs=[IN_VMEM, IN_VMEM],
        out_shape=jax.ShapeDtypeStruct((toks, width), F32),
        compiler_params=pltpu.CompilerParams(vmem_limit_bytes=SCOPED),
        name="combine",
    )(pick, rows)


def backward(go, wd, act, slope, wg, wu, part, parts, cap):
    rows, width = go.shape
    hidden = wd.shape[1]
    chunk = width // parts
    shape = (rows // cap, cap, width)

    def body(go_h, wd_h, act_h, slope_h, wg_h, wu_h, dxs_h, da_h, db_h, *scratch):
        go_ref, wd_ref, act_ref, slope_ref, wg_ref, wu_ref, dxs_ref, da_ref, db_ref, sems = scratch
        steps = hidden // part

        def load(n, src, dst):
            return pltpu.make_async_copy(src, dst, sems.at[n])

        def columns(n):
            here = pl.ds(n * part, part)
            return load(8 + n, wd_h.at[:, here], wd_ref.at[:, here])

        wd_in = [columns(n) for n in range(steps)]
        go_in, slope_in, act_in = load(0, go_h, go_ref), load(1, slope_h, slope_ref), load(2, act_h, act_ref)
        later = [load(3, wg_h, wg_ref), load(4, wu_h, wu_ref)]
        keep = [load(5, da_ref, da_h), load(6, db_ref, db_h)]

        def send(i):
            here = pl.ds(i, chunk)
            return pltpu.make_async_copy(
                dxs_ref.at[:, :, here], dxs_h.at[:, :, here], sems.at[8 + steps + i // chunk]
            )

        go_in.start()
        wd_in[0].start()
        slope_in.start()
        act_in.start()
        go_in.wait()
        wd_in[0].wait()
        for copy in wd_in[1:] + later:
            copy.start()
        slope_in.wait()
        act_in.wait()
        for i in range(0, hidden, part):
            if i > 0:
                wd_in[i // part].wait()
            dh = mm(go_ref[...], wd_ref[:, i : i + part], ((1,), (0,)))
            da_ref[:, i : i + part] = (dh * slope_ref[:, i : i + part]).astype(BF16)
            db_ref[:, i : i + part] = (dh * act_ref[:, i : i + part]).astype(BF16)
        for copy in later:
            copy.wait()
        for i in range(0, width, chunk):
            dxs = mm(da_ref[...], wg_ref[i : i + chunk, :], ((1,), (1,))) + mm(
                db_ref[...], wu_ref[i : i + chunk, :], ((1,), (1,))
            )
            dxs_ref[:, :, i : i + chunk] = dxs.reshape(shape[0], cap, chunk).astype(BF16)
            send(i).start()
        for copy in keep:
            copy.start()
        for i in range(0, width, chunk):
            send(i).wait()
        for copy in keep:
            copy.wait()

    return pl.pallas_call(
        body,
        in_specs=[IN_HBM] * 6,
        out_specs=[IN_HBM] * 3,
        out_shape=[
            pltpu.HBM(shape, BF16),
            pltpu.HBM((rows, hidden), BF16),
            pltpu.HBM((rows, hidden), BF16),
        ],
        scratch_shapes=[
            pltpu.VMEM((rows, width), BF16),
            pltpu.VMEM((width, hidden), BF16),
            pltpu.VMEM((rows, hidden), F32),
            pltpu.VMEM((rows, hidden), F32),
            pltpu.VMEM((width, hidden), BF16),
            pltpu.VMEM((width, hidden), BF16),
            pltpu.VMEM(shape, BF16),
            pltpu.VMEM((rows, hidden), BF16),
            pltpu.VMEM((rows, hidden), BF16),
            pltpu.SemaphoreType.DMA((8 + hidden // part + parts,)),
        ],
        compiler_params=pltpu.CompilerParams(vmem_limit_bytes=4 * SCOPED),
        name="backward",
    )(*(pltpu.with_memory_space_constraint(v, pltpu.HBM) for v in (go, wd, act, slope, wg, wu)))


def per_device(hidden_in, out_grad, route_prob, route_ids, w_gate, w_up, w_down):
    tok_count, top_count = route_ids.shape
    width = hidden_in.shape[1]
    depth = lax.axis_size("z")
    peers = depth * PLANE
    half = w_gate.shape[2]
    slot_cap = max(2, 12 * tok_count // peers)
    total_slots = peers * slot_cap
    swap = [(0, 1), (1, 0)]

    column, came_from = along_z(prepare(hidden_in, route_ids.T, route_prob.T), depth)
    g_column, _ = along_z(narrow(out_grad, column[-3:-1]), depth)
    block = depth * slot_cap
    send_x, weigh = fill_x(
        column, came_from, lax.axis_index("z").reshape(1), top_count, slot_cap, width, 4, g_column[1:3]
    )

    def in_plane(rows):
        return lax.all_to_all(
            rows.reshape(PLANE, block, width), ("y", "x"), split_axis=0, concat_axis=0, tiled=True
        ).reshape(total_slots, width)

    xs = in_plane(send_x)
    send_g = fill_g(weigh, g_column, 4)
    send_g, xs = lax.optimization_barrier((send_g, xs))
    go = in_plane(send_g)

    slot = lax.broadcasted_iota(jnp.int32, (total_slots, 1), 0)
    peer = slot // slot_cap
    slot_expert = (peer % depth) * PLANE + peer // depth
    named, _ = named_by(slot_expert, route_ids.T, None)
    rank = mm(named.astype(BF16), before(tok_count, tok_count), ((1,), (0,)))
    pick = ((named > 0.0) & (rank == (slot % slot_cap).astype(F32))).astype(BF16)

    def both(w):
        return jnp.concatenate([w[0], lax.ppermute(w[0], "dp", swap)], axis=1)

    wg, wu, wd = both(w_gate), both(w_up), both(w_down)

    act, slope, hid = activations(xs, wg, wu, 256)
    dxs, da, db = backward(go, wd, act, slope, wg, wu, 256, 4, slot_cap)
    returned = lax.all_to_all(dxs, ("y", "x", "z"), split_axis=0, concat_axis=0, tiled=True)

    def grad(rows, hidden):
        mine = mm(rows, hidden[:, :half], ((0,), (0,))).astype(BF16)
        other = mm(rows, hidden[:, half:], ((0,), (0,))).astype(BF16)
        got = lax.ppermute(other, "dp", swap)
        return (mine.astype(F32) + got.astype(F32)).astype(BF16)[None]

    grads = (grad(xs, da), grad(xs, db), grad(go, hid))
    input_grad = combine(pick, returned, 4)
    return (input_grad, grads[0], grads[1], grads[2])


def solution(mesh):
    grid = Mesh(mesh.devices.reshape(-1, 4, 4, 2), ("z", "y", "x", "dp"))
    tok = P(("z", "y", "x", "dp"), None)
    wts = P(("z", "y", "x"), None, "dp")
    return jax.shard_map(
        per_device,
        mesh=grid,
        in_specs=(tok, tok, tok, tok, wts, wts, wts),
        out_specs=(tok, wts, wts, wts),
        check_vma=False,
    )
```

```python
import jax
import jax.numpy as jnp
from jax import lax
from jax.experimental import pallas as pl
from jax.experimental.pallas import tpu as pltpu
from jax.sharding import Mesh, PartitionSpec as P

F32 = jnp.float32
BF16 = jnp.bfloat16
PLANE = 16
LANES = 128
SCOPED = 8 << 20
IN_HBM = pl.BlockSpec(memory_space=pltpu.HBM)
IN_VMEM = pl.BlockSpec(memory_space=pltpu.VMEM)


def mm(a, b, dims):
    return lax.dot_general(a, b, ((dims[0], dims[1]), ((), ())), preferred_element_type=F32)


def before(count, block):
    i = lax.broadcasted_iota(jnp.int32, (count, count), 0)
    j = lax.broadcasted_iota(jnp.int32, (count, count), 1)
    return ((i < j) & (i // block == j // block)).astype(BF16)


def named_by(expert, ids_t, prob_t):
    named = jnp.zeros(jnp.broadcast_shapes(expert.shape, (1, ids_t.shape[1])), F32)
    prob = named
    for k in range(ids_t.shape[0]):
        hit = expert == ids_t[k][None, :]
        named = jnp.where(hit, 1.0, named)
        if prob_t is not None:
            prob = jnp.where(hit, prob_t[k][None, :], prob)
    return named, prob


def along_z(rows, depth, first):
    found = {0: rows}
    ahead = behind = rows
    for step in range(1, depth // 2 + 1):
        ahead = lax.ppermute(ahead, "z", [(i, (i + first) % depth) for i in range(depth)])
        found[-first * step % depth] = ahead
        if step < depth - step:
            behind = lax.ppermute(behind, "z", [(i, (i - first) % depth) for i in range(depth)])
            found[first * step % depth] = behind
    return found


def iota(shape, dim):
    return lax.broadcasted_iota(jnp.int32, shape, dim)


def prepare(x, ids_t, prob_t):
    toks, width = x.shape
    top = ids_t.shape[0]

    def body(x_ref, ids_ref, prob_ref, out_ref):
        out_ref[:, :width] = x_ref[...].astype(BF16)
        small = jnp.concatenate([ids_ref[...].astype(F32), prob_ref[...]], axis=0).astype(BF16)
        place = (iota((2 * top, LANES), 0) == iota((2 * top, LANES), 1)).astype(F32).astype(BF16)
        out_ref[:, width:] = mm(small, place, ((0,), (0,))).astype(BF16)

    return pl.pallas_call(
        body,
        out_specs=IN_VMEM,
        out_shape=jax.ShapeDtypeStruct((toks, width + LANES), BF16),
        name="prepare",
    )(x, ids_t, prob_t)


def narrow(x, after):
    def body(x_ref, *refs):
        refs[-1][...] = x_ref[...].astype(BF16)

    return pl.pallas_call(
        body,
        in_specs=[IN_VMEM] * (1 + len(after)),
        out_specs=IN_VMEM,
        out_shape=jax.ShapeDtypeStruct(x.shape, BF16),
        compiler_params=pltpu.CompilerParams(vmem_limit_bytes=SCOPED),
        name="narrow",
    )(x, *after)


def fill_x(blocks, offsets, z, top, cap, width, parts, after):
    toks = blocks[0].shape[0]
    depth = len(blocks)
    cols = depth * toks
    rows = depth * cap
    slots = PLANE * rows
    chunk = width // parts

    def body(z_ref, *refs):
        out_ref, weigh_ref, pick_ref, buf_ref, sems = refs[depth + len(after) :]
        refs = refs[:depth]
        if True:
            me = z_ref[0]
            meta = jnp.concatenate([ref[:, width:] for ref in refs], axis=0)
            take = (iota((2 * top, LANES), 0) == iota((2 * top, LANES), 1)).astype(F32).astype(BF16)
            small = mm(take, meta, ((1,), (1,)))
            expert = (iota((PLANE, cols), 0) + me * PLANE).astype(F32)
            named = jnp.zeros((PLANE, cols), F32)
            prob = jnp.zeros((PLANE, cols), F32)
            for k in range(top):
                hit = small[k : k + 1] == expert
                named = jnp.where(hit, 1.0, named)
                prob = jnp.where(hit, small[top + k : top + k + 1], prob)
            i, j = iota((cols, cols), 0), iota((cols, cols), 1)
            start = jnp.zeros((cols, cols), jnp.int32)
            for b in range(1, depth):
                start = jnp.where(j >= b * toks, b * toks, start)
            earlier = jnp.where((i < j) & (i >= start), 1.0, 0.0).astype(BF16)
            rank = mm(named.astype(BF16), earlier, ((1,), (0,)))
            rank = jnp.where(named > 0.0, rank, -64.0 * depth)
            row, col = iota((rows, cols), 0), iota((rows, cols), 1)
            source = jnp.zeros((rows, cols), jnp.int32)
            for b in range(depth):
                source = jnp.where(col >= b * toks, (me + offsets[b]) & (depth - 1), source)
            wanted = (row - source * cap).astype(F32)
            for e in range(PLANE):
                chosen = (rank[e : e + 1] == wanted)
                pick_ref[e * rows : (e + 1) * rows] = jnp.where(chosen, 1.0, 0.0).astype(BF16)
                weigh_ref[e * rows : (e + 1) * rows] = jnp.where(chosen, prob[e : e + 1], 0.0).astype(BF16)

        def send(i):
            here = pl.ds(i, chunk)
            return pltpu.make_async_copy(buf_ref.at[:, here], out_ref.at[:, here], sems.at[i // chunk])

        for i in range(0, width, chunk):
            x = jnp.concatenate([ref[:, i : i + chunk] for ref in refs], axis=0)
            buf_ref[:, i : i + chunk] = mm(pick_ref[...], x, ((1,), (0,))).astype(BF16)
            send(i).start()
        for i in range(0, width, chunk):
            send(i).wait()

    return pl.pallas_call(
        body,
        in_specs=[pl.BlockSpec(memory_space=pltpu.SMEM)] + [IN_VMEM] * (depth + len(after)),
        out_specs=[IN_HBM, IN_VMEM],
        scratch_shapes=[
            pltpu.VMEM((slots, cols), BF16),
            pltpu.VMEM((slots, width), BF16),
            pltpu.SemaphoreType.DMA((parts,)),
        ],
        out_shape=[pltpu.HBM((slots, width), BF16), pltpu.VMEM((slots, cols), BF16)],
        compiler_params=pltpu.CompilerParams(vmem_limit_bytes=SCOPED),
        name="fill_x",
    )(z, *blocks, *after)


def fill_g(weigh, blocks, parts):
    toks, width = blocks[0].shape
    slots, cols = weigh.shape
    chunk = width // parts

    def body(weigh_ref, *refs):
        refs, (out_ref, buf_ref, sems) = refs[:-3], refs[-3:]

        def send(i):
            here = pl.ds(i, chunk)
            return pltpu.make_async_copy(buf_ref.at[:, here], out_ref.at[:, here], sems.at[i // chunk])

        for i in range(0, width, chunk):
            g = jnp.concatenate([ref[:, i : i + chunk] for ref in refs], axis=0)
            buf_ref[:, i : i + chunk] = mm(weigh_ref[...], g, ((1,), (0,))).astype(BF16)
            send(i).start()
        for i in range(0, width, chunk):
            send(i).wait()

    return pl.pallas_call(
        body,
        in_specs=[IN_VMEM] * (1 + len(blocks)),
        out_specs=IN_HBM,
        scratch_shapes=[pltpu.VMEM((slots, width), BF16), pltpu.SemaphoreType.DMA((parts,))],
        out_shape=pltpu.HBM((slots, width), BF16),
        compiler_params=pltpu.CompilerParams(vmem_limit_bytes=SCOPED),
        name="fill_g",
    )(weigh, *blocks)


def activations(xs, wg, wu, part):
    rows, width = xs.shape
    hidden = wg.shape[1]

    def body(x_ref, wg_ref, wu_ref, act_h, slope_h, hid_h, act_ref, slope_ref, hid_ref, sems):
        for i in range(0, hidden, part):
            a = mm(x_ref[...], wg_ref[:, i : i + part], ((1,), (0,)))
            b = mm(x_ref[...], wu_ref[:, i : i + part], ((1,), (0,)))
            sig = 1.0 / (1.0 + jnp.exp(-a))
            act = a * sig
            act_ref[:, i : i + part] = act
            slope_ref[:, i : i + part] = b * sig * (1.0 + a * (1.0 - sig))
            hid_ref[:, i : i + part] = (act * b).astype(BF16)
        copies = [
            pltpu.make_async_copy(src, dst, sems.at[i])
            for i, (src, dst) in enumerate([(act_ref, act_h), (slope_ref, slope_h), (hid_ref, hid_h)])
        ]
        for copy in copies:
            copy.start()
        for copy in copies:
            copy.wait()

    return pl.pallas_call(
        body,
        in_specs=[IN_VMEM] * 3,
        out_specs=[IN_HBM] * 3,
        out_shape=[
            pltpu.HBM((rows, hidden), F32),
            pltpu.HBM((rows, hidden), F32),
            pltpu.HBM((rows, hidden), BF16),
        ],
        scratch_shapes=[
            pltpu.VMEM((rows, hidden), F32),
            pltpu.VMEM((rows, hidden), F32),
            pltpu.VMEM((rows, hidden), BF16),
            pltpu.SemaphoreType.DMA((3,)),
        ],
        compiler_params=pltpu.CompilerParams(vmem_limit_bytes=2 * SCOPED),
        name="activations",
    )(pltpu.with_memory_space_constraint(xs, pltpu.VMEM), wg, wu)


def combine(pick, rows, parts):
    slots, toks = pick.shape
    peers, cap, width = rows.shape
    chunk = width // parts

    def body(pick_ref, rows_ref, out_ref):
        for i in range(0, width, chunk):
            part = rows_ref[:, :, i : i + chunk].astype(F32).reshape(slots, chunk).astype(BF16)
            out_ref[:, i : i + chunk] = mm(pick_ref[...], part, ((0,), (0,)))

    return pl.pallas_call(
        body,
        in_specs=[IN_VMEM, IN_VMEM],
        out_shape=jax.ShapeDtypeStruct((toks, width), F32),
        compiler_params=pltpu.CompilerParams(vmem_limit_bytes=SCOPED),
        name="combine",
    )(pick, rows)


def backward(go, wd, act, slope, wg, wu, part, parts, cap):
    rows, width = go.shape
    hidden = wd.shape[1]
    chunk = width // parts
    shape = (rows // cap, cap, width)

    def body(go_h, wd_h, act_h, slope_h, wg_h, wu_h, dxs_h, da_h, db_h, *scratch):
        go_ref, wd_ref, act_ref, slope_ref, wg_ref, wu_ref, dxs_ref, da_ref, db_ref, sems = scratch
        steps = hidden // part

        def load(n, src, dst):
            return pltpu.make_async_copy(src, dst, sems.at[n])

        def columns(n):
            here = pl.ds(n * part, part)
            return load(8 + n, wd_h.at[:, here], wd_ref.at[:, here])

        wd_in = [columns(n) for n in range(steps)]
        go_in, slope_in, act_in = load(0, go_h, go_ref), load(1, slope_h, slope_ref), load(2, act_h, act_ref)
        later = [load(3, wg_h, wg_ref), load(4, wu_h, wu_ref)]
        keep = [load(5, da_ref, da_h), load(6, db_ref, db_h)]

        def send(i):
            here = pl.ds(i, chunk)
            return pltpu.make_async_copy(
                dxs_ref.at[:, :, here], dxs_h.at[:, :, here], sems.at[8 + steps + i // chunk]
            )

        go_in.start()
        wd_in[0].start()
        slope_in.start()
        act_in.start()
        go_in.wait()
        wd_in[0].wait()
        for copy in wd_in[1:] + later:
            copy.start()
        slope_in.wait()
        act_in.wait()
        for i in range(0, hidden, part):
            if i > 0:
                wd_in[i // part].wait()
            dh = mm(go_ref[...], wd_ref[:, i : i + part], ((1,), (0,)))
            da_ref[:, i : i + part] = (dh * slope_ref[:, i : i + part]).astype(BF16)
            db_ref[:, i : i + part] = (dh * act_ref[:, i : i + part]).astype(BF16)
        for copy in keep:
            copy.start()
        for copy in later:
            copy.wait()
        for i in range(0, width, chunk):
            dxs = mm(da_ref[...], wg_ref[i : i + chunk, :], ((1,), (1,))) + mm(
                db_ref[...], wu_ref[i : i + chunk, :], ((1,), (1,))
            )
            dxs_ref[:, :, i : i + chunk] = dxs.reshape(shape[0], cap, chunk).astype(BF16)
            send(i).start()
        for i in range(0, width, chunk):
            send(i).wait()
        for copy in keep:
            copy.wait()

    return pl.pallas_call(
        body,
        in_specs=[IN_HBM] * 6,
        out_specs=[IN_HBM] * 3,
        out_shape=[
            pltpu.HBM(shape, BF16),
            pltpu.HBM((rows, hidden), BF16),
            pltpu.HBM((rows, hidden), BF16),
        ],
        scratch_shapes=[
            pltpu.VMEM((rows, width), BF16),
            pltpu.VMEM((width, hidden), BF16),
            pltpu.VMEM((rows, hidden), F32),
            pltpu.VMEM((rows, hidden), F32),
            pltpu.VMEM((width, hidden), BF16),
            pltpu.VMEM((width, hidden), BF16),
            pltpu.VMEM(shape, BF16),
            pltpu.VMEM((rows, hidden), BF16),
            pltpu.VMEM((rows, hidden), BF16),
            pltpu.SemaphoreType.DMA((8 + hidden // part + parts,)),
        ],
        compiler_params=pltpu.CompilerParams(vmem_limit_bytes=4 * SCOPED),
        name="backward",
    )(*(pltpu.with_memory_space_constraint(v, pltpu.HBM) for v in (go, wd, act, slope, wg, wu)))


def per_device(hidden_in, out_grad, route_prob, route_ids, w_gate, w_up, w_down):
    tok_count, top_count = route_ids.shape
    width = hidden_in.shape[1]
    depth = lax.axis_size("z")
    peers = depth * PLANE
    half = w_gate.shape[2]
    slot_cap = max(2, 12 * tok_count // peers)
    total_slots = peers * slot_cap
    swap = [(0, 1), (1, 0)]

    x_at = along_z(prepare(hidden_in, route_ids.T, route_prob.T), depth, 1)
    last = depth // 2
    g_at = along_z(narrow(out_grad, [x_at[depth + 1 - last]]), depth, -1)
    came_from = sorted(x_at)
    column = [x_at[offset] for offset in came_from]
    g_column = [g_at[offset] for offset in came_from]
    block = depth * slot_cap
    send_x, weigh = fill_x(
        column, came_from, lax.axis_index("z").reshape(1), top_count, slot_cap, width, 4, [g_at[1]]
    )

    def in_plane(rows):
        return lax.all_to_all(
            rows.reshape(PLANE, block, width), ("y", "x"), split_axis=0, concat_axis=0, tiled=True
        ).reshape(total_slots, width)

    xs = in_plane(send_x)
    send_g = fill_g(weigh, g_column, 4)
    send_g, xs = lax.optimization_barrier((send_g, xs))
    go = in_plane(send_g)

    slot = lax.broadcasted_iota(jnp.int32, (total_slots, 1), 0)
    peer = slot // slot_cap
    slot_expert = (peer % depth) * PLANE + peer // depth
    named, _ = named_by(slot_expert, route_ids.T, None)
    rank = mm(named.astype(BF16), before(tok_count, tok_count), ((1,), (0,)))
    pick = ((named > 0.0) & (rank == (slot % slot_cap).astype(F32))).astype(BF16)

    def both(w):
        return jnp.concatenate([w[0], lax.ppermute(w[0], "dp", swap)], axis=1)

    wg, wu, wd = both(w_gate), both(w_up), both(w_down)

    act, slope, hid = activations(xs, wg, wu, 256)
    dxs, da, db = backward(go, wd, act, slope, wg, wu, 256, 4, slot_cap)
    returned = lax.all_to_all(dxs, ("y", "x", "z"), split_axis=0, concat_axis=0, tiled=True)

    def grad(rows, hidden):
        mine = mm(rows, hidden[:, :half], ((0,), (0,))).astype(BF16)
        other = mm(rows, hidden[:, half:], ((0,), (0,))).astype(BF16)
        got = lax.ppermute(other, "dp", swap)
        return (mine.astype(F32) + got.astype(F32)).astype(BF16)[None]

    grads = (grad(xs, da), grad(xs, db), grad(go, hid))
    input_grad = combine(pick, returned, 4)
    return (input_grad, grads[0], grads[1], grads[2])


def solution(mesh):
    grid = Mesh(mesh.devices.reshape(-1, 4, 4, 2), ("z", "y", "x", "dp"))
    tok = P(("z", "y", "x", "dp"), None)
    wts = P(("z", "y", "x"), None, "dp")
    return jax.shard_map(
        per_device,
        mesh=grid,
        in_specs=(tok, tok, tok, tok, wts, wts, wts),
        out_specs=(tok, wts, wts, wts),
        check_vma=False,
    )
```

```python
import jax
import jax.numpy as jnp
from jax import lax
from jax.experimental import pallas as pl
from jax.experimental.pallas import tpu as pltpu
from jax.sharding import Mesh, PartitionSpec as P

F32 = jnp.float32
BF16 = jnp.bfloat16
PLANE = 16
LANES = 128
SCOPED = 8 << 20
IN_HBM = pl.BlockSpec(memory_space=pltpu.HBM)
IN_VMEM = pl.BlockSpec(memory_space=pltpu.VMEM)


def mm(a, b, dims):
    return lax.dot_general(a, b, ((dims[0], dims[1]), ((), ())), preferred_element_type=F32)


def before(count, block):
    i = lax.broadcasted_iota(jnp.int32, (count, count), 0)
    j = lax.broadcasted_iota(jnp.int32, (count, count), 1)
    return ((i < j) & (i // block == j // block)).astype(BF16)


def named_by(expert, ids_t, prob_t):
    named = jnp.zeros(jnp.broadcast_shapes(expert.shape, (1, ids_t.shape[1])), F32)
    prob = named
    for k in range(ids_t.shape[0]):
        hit = expert == ids_t[k][None, :]
        named = jnp.where(hit, 1.0, named)
        if prob_t is not None:
            prob = jnp.where(hit, prob_t[k][None, :], prob)
    return named, prob


def along_z(rows, depth, first):
    found = {0: rows}
    ahead = behind = rows
    for step in range(1, depth // 2 + 1):
        ahead = lax.ppermute(ahead, "z", [(i, (i + first) % depth) for i in range(depth)])
        found[-first * step % depth] = ahead
        if step < depth - step:
            behind = lax.ppermute(behind, "z", [(i, (i - first) % depth) for i in range(depth)])
            found[first * step % depth] = behind
    return found


def iota(shape, dim):
    return lax.broadcasted_iota(jnp.int32, shape, dim)


def prepare(x, ids_t, prob_t):
    toks, width = x.shape
    top = ids_t.shape[0]

    def body(x_ref, ids_ref, prob_ref, out_ref):
        out_ref[:, :width] = x_ref[...].astype(BF16)
        small = jnp.concatenate([ids_ref[...].astype(F32), prob_ref[...]], axis=0).astype(BF16)
        place = (iota((2 * top, LANES), 0) == iota((2 * top, LANES), 1)).astype(F32).astype(BF16)
        out_ref[:, width:] = mm(small, place, ((0,), (0,))).astype(BF16)

    return pl.pallas_call(
        body,
        out_specs=IN_VMEM,
        out_shape=jax.ShapeDtypeStruct((toks, width + LANES), BF16),
        name="prepare",
    )(x, ids_t, prob_t)


def narrow(x, after):
    def body(x_ref, *refs):
        refs[-1][...] = x_ref[...].astype(BF16)

    return pl.pallas_call(
        body,
        in_specs=[IN_VMEM] * (1 + len(after)),
        out_specs=IN_VMEM,
        out_shape=jax.ShapeDtypeStruct(x.shape, BF16),
        compiler_params=pltpu.CompilerParams(vmem_limit_bytes=SCOPED),
        name="narrow",
    )(x, *after)


def fill_x(blocks, offsets, z, top, cap, width, parts, after):
    toks = blocks[0].shape[0]
    depth = len(blocks)
    cols = depth * toks
    rows = depth * cap
    slots = PLANE * rows
    chunk = width // parts

    def body(z_ref, *refs):
        out_ref, weigh_ref, pick_ref, buf_ref, sems = refs[depth + len(after) :]
        refs = refs[:depth]
        if True:
            me = z_ref[0]
            meta = jnp.concatenate([ref[:, width:] for ref in refs], axis=0)
            take = (iota((2 * top, LANES), 0) == iota((2 * top, LANES), 1)).astype(F32).astype(BF16)
            small = mm(take, meta, ((1,), (1,)))
            expert = (iota((PLANE, cols), 0) + me * PLANE).astype(F32)
            named = jnp.zeros((PLANE, cols), F32)
            prob = jnp.zeros((PLANE, cols), F32)
            for k in range(top):
                hit = small[k : k + 1] == expert
                named = jnp.where(hit, 1.0, named)
                prob = jnp.where(hit, small[top + k : top + k + 1], prob)
            i, j = iota((cols, cols), 0), iota((cols, cols), 1)
            start = jnp.zeros((cols, cols), jnp.int32)
            for b in range(1, depth):
                start = jnp.where(j >= b * toks, b * toks, start)
            earlier = jnp.where((i < j) & (i >= start), 1.0, 0.0).astype(BF16)
            rank = mm(named.astype(BF16), earlier, ((1,), (0,)))
            rank = jnp.where(named > 0.0, rank, -64.0 * depth)
            row, col = iota((rows, cols), 0), iota((rows, cols), 1)
            source = jnp.zeros((rows, cols), jnp.int32)
            for b in range(depth):
                source = jnp.where(col >= b * toks, (me + offsets[b]) & (depth - 1), source)
            wanted = (row - source * cap).astype(F32)
            for e in range(PLANE):
                chosen = (rank[e : e + 1] == wanted)
                pick_ref[e * rows : (e + 1) * rows] = jnp.where(chosen, 1.0, 0.0).astype(BF16)
                weigh_ref[e * rows : (e + 1) * rows] = jnp.where(chosen, prob[e : e + 1], 0.0).astype(BF16)

        def send(i):
            here = pl.ds(i, chunk)
            return pltpu.make_async_copy(buf_ref.at[:, here], out_ref.at[:, here], sems.at[i // chunk])

        for i in range(0, width, chunk):
            x = jnp.concatenate([ref[:, i : i + chunk] for ref in refs], axis=0)
            buf_ref[:, i : i + chunk] = mm(pick_ref[...], x, ((1,), (0,))).astype(BF16)
            send(i).start()
        for i in range(0, width, chunk):
            send(i).wait()

    return pl.pallas_call(
        body,
        in_specs=[pl.BlockSpec(memory_space=pltpu.SMEM)] + [IN_VMEM] * (depth + len(after)),
        out_specs=[IN_HBM, IN_VMEM],
        scratch_shapes=[
            pltpu.VMEM((slots, cols), BF16),
            pltpu.VMEM((slots, width), BF16),
            pltpu.SemaphoreType.DMA((parts,)),
        ],
        out_shape=[pltpu.HBM((slots, width), BF16), pltpu.VMEM((slots, cols), BF16)],
        compiler_params=pltpu.CompilerParams(vmem_limit_bytes=SCOPED),
        name="fill_x",
    )(z, *blocks, *after)


def fill_g(weigh, blocks, parts):
    toks, width = blocks[0].shape
    slots, cols = weigh.shape
    chunk = width // parts

    def body(weigh_ref, *refs):
        refs, (out_ref, buf_ref, sems) = refs[:-3], refs[-3:]

        def send(i):
            here = pl.ds(i, chunk)
            return pltpu.make_async_copy(buf_ref.at[:, here], out_ref.at[:, here], sems.at[i // chunk])

        for i in range(0, width, chunk):
            g = jnp.concatenate([ref[:, i : i + chunk] for ref in refs], axis=0)
            buf_ref[:, i : i + chunk] = mm(weigh_ref[...], g, ((1,), (0,))).astype(BF16)
            send(i).start()
        for i in range(0, width, chunk):
            send(i).wait()

    return pl.pallas_call(
        body,
        in_specs=[IN_VMEM] * (1 + len(blocks)),
        out_specs=IN_HBM,
        scratch_shapes=[pltpu.VMEM((slots, width), BF16), pltpu.SemaphoreType.DMA((parts,))],
        out_shape=pltpu.HBM((slots, width), BF16),
        compiler_params=pltpu.CompilerParams(vmem_limit_bytes=SCOPED),
        name="fill_g",
    )(weigh, *blocks)


def activations(xs, wg, wu, part):
    rows, width = xs.shape
    hidden = wg.shape[1]

    def body(x_ref, wg_ref, wu_ref, act_h, slope_h, hid_h, act_ref, slope_ref, hid_ref, sems):
        for i in range(0, hidden, part):
            a = mm(x_ref[...], wg_ref[:, i : i + part], ((1,), (0,)))
            b = mm(x_ref[...], wu_ref[:, i : i + part], ((1,), (0,)))
            sig = 1.0 / (1.0 + jnp.exp(-a))
            act = a * sig
            act_ref[:, i : i + part] = act
            slope_ref[:, i : i + part] = b * sig * (1.0 + a * (1.0 - sig))
            hid_ref[:, i : i + part] = (act * b).astype(BF16)
        copies = [
            pltpu.make_async_copy(src, dst, sems.at[i])
            for i, (src, dst) in enumerate([(act_ref, act_h), (slope_ref, slope_h), (hid_ref, hid_h)])
        ]
        for copy in copies:
            copy.start()
        for copy in copies:
            copy.wait()

    return pl.pallas_call(
        body,
        in_specs=[IN_VMEM] * 3,
        out_specs=[IN_HBM] * 3,
        out_shape=[
            pltpu.HBM((rows, hidden), F32),
            pltpu.HBM((rows, hidden), F32),
            pltpu.HBM((rows, hidden), BF16),
        ],
        scratch_shapes=[
            pltpu.VMEM((rows, hidden), F32),
            pltpu.VMEM((rows, hidden), F32),
            pltpu.VMEM((rows, hidden), BF16),
            pltpu.SemaphoreType.DMA((3,)),
        ],
        compiler_params=pltpu.CompilerParams(vmem_limit_bytes=2 * SCOPED),
        name="activations",
    )(pltpu.with_memory_space_constraint(xs, pltpu.VMEM), wg, wu)


def combine(pick, rows, parts):
    slots, toks = pick.shape
    peers, cap, width = rows.shape
    chunk = width // parts

    def body(pick_ref, rows_ref, out_ref):
        for i in range(0, width, chunk):
            part = rows_ref[:, :, i : i + chunk].astype(F32).reshape(slots, chunk).astype(BF16)
            out_ref[:, i : i + chunk] = mm(pick_ref[...], part, ((0,), (0,)))

    return pl.pallas_call(
        body,
        in_specs=[IN_VMEM, IN_VMEM],
        out_shape=jax.ShapeDtypeStruct((toks, width), F32),
        compiler_params=pltpu.CompilerParams(vmem_limit_bytes=SCOPED),
        name="combine",
    )(pick, rows)


def backward(go, wd, act, slope, wg, wu, part, parts, cap):
    rows, width = go.shape
    hidden = wd.shape[1]
    chunk = width // parts
    shape = (rows // cap, cap, width)

    def body(go_h, wd_h, act_h, slope_h, wg_h, wu_h, dxs_h, da_h, db_h, *scratch):
        go_ref, wd_ref, act_ref, slope_ref, wg_ref, wu_ref, dxs_ref, da_ref, db_ref, sems = scratch
        steps = hidden // part

        def load(n, src, dst):
            return pltpu.make_async_copy(src, dst, sems.at[n])

        def columns(n):
            here = pl.ds(n * part, part)
            return load(8 + n, wd_h.at[:, here], wd_ref.at[:, here])

        wd_in = [columns(n) for n in range(steps)]
        go_in, slope_in, act_in = load(0, go_h, go_ref), load(1, slope_h, slope_ref), load(2, act_h, act_ref)
        later = [load(3, wg_h, wg_ref), load(4, wu_h, wu_ref)]
        keep = [load(5, da_ref, da_h), load(6, db_ref, db_h)]

        def send(i):
            here = pl.ds(i, chunk)
            return pltpu.make_async_copy(
                dxs_ref.at[:, :, here], dxs_h.at[:, :, here], sems.at[8 + steps + i // chunk]
            )

        go_in.start()
        wd_in[0].start()
        go_in.wait()
        wd_in[0].wait()
        for copy in [slope_in, act_in] + wd_in[1:] + later:
            copy.start()
        for i in range(0, hidden, part):
            if i > 0:
                wd_in[i // part].wait()
            dh = mm(go_ref[...], wd_ref[:, i : i + part], ((1,), (0,)))
            if i == 0:
                slope_in.wait()
                act_in.wait()
            da_ref[:, i : i + part] = (dh * slope_ref[:, i : i + part]).astype(BF16)
            db_ref[:, i : i + part] = (dh * act_ref[:, i : i + part]).astype(BF16)
        for copy in keep:
            copy.start()
        for copy in later:
            copy.wait()
        for i in range(0, width, chunk):
            dxs = mm(da_ref[...], wg_ref[i : i + chunk, :], ((1,), (1,))) + mm(
                db_ref[...], wu_ref[i : i + chunk, :], ((1,), (1,))
            )
            dxs_ref[:, :, i : i + chunk] = dxs.reshape(shape[0], cap, chunk).astype(BF16)
            send(i).start()
        for i in range(0, width, chunk):
            send(i).wait()
        for copy in keep:
            copy.wait()

    return pl.pallas_call(
        body,
        in_specs=[IN_HBM] * 6,
        out_specs=[IN_HBM] * 3,
        out_shape=[
            pltpu.HBM(shape, BF16),
            pltpu.HBM((rows, hidden), BF16),
            pltpu.HBM((rows, hidden), BF16),
        ],
        scratch_shapes=[
            pltpu.VMEM((rows, width), BF16),
            pltpu.VMEM((width, hidden), BF16),
            pltpu.VMEM((rows, hidden), F32),
            pltpu.VMEM((rows, hidden), F32),
            pltpu.VMEM((width, hidden), BF16),
            pltpu.VMEM((width, hidden), BF16),
            pltpu.VMEM(shape, BF16),
            pltpu.VMEM((rows, hidden), BF16),
            pltpu.VMEM((rows, hidden), BF16),
            pltpu.SemaphoreType.DMA((8 + hidden // part + parts,)),
        ],
        compiler_params=pltpu.CompilerParams(vmem_limit_bytes=4 * SCOPED),
        name="backward",
    )(*(pltpu.with_memory_space_constraint(v, pltpu.HBM) for v in (go, wd, act, slope, wg, wu)))


def per_device(hidden_in, out_grad, route_prob, route_ids, w_gate, w_up, w_down):
    tok_count, top_count = route_ids.shape
    width = hidden_in.shape[1]
    depth = lax.axis_size("z")
    peers = depth * PLANE
    half = w_gate.shape[2]
    slot_cap = max(2, 12 * tok_count // peers)
    total_slots = peers * slot_cap
    swap = [(0, 1), (1, 0)]

    x_at = along_z(prepare(hidden_in, route_ids.T, route_prob.T), depth, 1)
    last = depth // 2
    g_at = along_z(narrow(out_grad, [x_at[depth + 1 - last]]), depth, -1)
    came_from = sorted(x_at)
    column = [x_at[offset] for offset in came_from]
    g_column = [g_at[offset] for offset in came_from]
    block = depth * slot_cap
    send_x, weigh = fill_x(
        column, came_from, lax.axis_index("z").reshape(1), top_count, slot_cap, width, 4, [g_at[1]]
    )

    def in_plane(rows):
        return lax.all_to_all(
            rows.reshape(PLANE, block, width), ("y", "x"), split_axis=0, concat_axis=0, tiled=True
        ).reshape(total_slots, width)

    xs = in_plane(send_x)
    send_g = fill_g(weigh, g_column, 4)
    send_g, xs = lax.optimization_barrier((send_g, xs))
    go = in_plane(send_g)

    slot = lax.broadcasted_iota(jnp.int32, (total_slots, 1), 0)
    peer = slot // slot_cap
    slot_expert = (peer % depth) * PLANE + peer // depth
    named, _ = named_by(slot_expert, route_ids.T, None)
    rank = mm(named.astype(BF16), before(tok_count, tok_count), ((1,), (0,)))
    pick = ((named > 0.0) & (rank == (slot % slot_cap).astype(F32))).astype(BF16)

    def both(w):
        return jnp.concatenate([w[0], lax.ppermute(w[0], "dp", swap)], axis=1)

    wg, wu, wd = both(w_gate), both(w_up), both(w_down)

    act, slope, hid = activations(xs, wg, wu, 256)
    dxs, da, db = backward(go, wd, act, slope, wg, wu, 256, 4, slot_cap)
    returned = lax.all_to_all(dxs, ("y", "x", "z"), split_axis=0, concat_axis=0, tiled=True)

    def grad(rows, hidden):
        mine = mm(rows, hidden[:, :half], ((0,), (0,))).astype(BF16)
        other = mm(rows, hidden[:, half:], ((0,), (0,))).astype(BF16)
        got = lax.ppermute(other, "dp", swap)
        return (mine.astype(F32) + got.astype(F32)).astype(BF16)[None]

    grads = (grad(xs, da), grad(xs, db), grad(go, hid))
    input_grad = combine(pick, returned, 4)
    return (input_grad, grads[0], grads[1], grads[2])


def solution(mesh):
    grid = Mesh(mesh.devices.reshape(-1, 4, 4, 2), ("z", "y", "x", "dp"))
    tok = P(("z", "y", "x", "dp"), None)
    wts = P(("z", "y", "x"), None, "dp")
    return jax.shard_map(
        per_device,
        mesh=grid,
        in_specs=(tok, tok, tok, tok, wts, wts, wts),
        out_specs=(tok, wts, wts, wts),
        check_vma=False,
    )
```
